32 devices in a mesh: fsdp: 4 (over z), ctx: 4 (over y, x), tensor: 2 (over core).
Axes of the slice: x: 2, y: 2, z: 4, core: 2. Of those that a mesh axis runs over, the one named last changes fastest.
Arguments:
- tokens: bfloat16 [8192, 2048], P(('fsdp', 'ctx')), may hold values from -6 to 6
- lengths: int32 [4, 3], P('fsdp'), may hold values from 1 to 1024, 2048 in all within a row
- attn_gain: bfloat16 [2048], P('fsdp'), may hold values from 0.5 to 1.5
- w_query: bfloat16 [2048, 2048], P('fsdp', 'tensor'), may hold values from -0.125 to 0.125
- w_key: bfloat16 [2048, 1024], P('fsdp', 'tensor'), may hold values from -0.125 to 0.125
- w_value: bfloat16 [2048, 1024], P('fsdp', 'tensor'), may hold values from -0.125 to 0.125
- w_out: bfloat16 [2048, 2048], P('fsdp', 'tensor'), may hold values from -0.5 to 0.5
- query_gain: bfloat16 [128], replicated, may hold values from 0.5 to 1.5
- key_gain: bfloat16 [128], replicated, may hold values from 0.5 to 1.5
- mlp_gain: bfloat16 [2048], P('fsdp'), may hold values from 0.5 to 1.5
- w_gate: bfloat16 [2048, 6144], P('fsdp', 'tensor'), may hold values from -0.125 to 0.125
- w_up: bfloat16 [2048, 6144], P('fsdp', 'tensor'), may hold values from -0.125 to 0.125
- w_down: bfloat16 [2048, 6144], P('fsdp', 'tensor'), may hold values from -0.078125 to 0.078125
- cotangent: bfloat16 [8192, 2048], P(('fsdp', 'ctx')), may hold values from -6 to 6
Outputs:
- layer_out: bfloat16 [8192, 2048], P(('fsdp', 'ctx'))
- grad_tokens: float32 [8192, 2048], P(('fsdp', 'ctx'))
- grad_attn_gain: float32 [2048], P('fsdp')
- grad_query: float32 [2048, 2048], P('fsdp', 'tensor')
- grad_key: float32 [2048, 1024], P('fsdp', 'tensor')
- grad_value: float32 [2048, 1024], P('fsdp', 'tensor')
- grad_out: float32 [2048, 2048], P('fsdp', 'tensor')
- grad_query_gain: float32 [128], replicated
- grad_key_gain: float32 [128], replicated
- grad_mlp_gain: float32 [2048], P('fsdp')
- grad_gate: float32 [2048, 6144], P('fsdp', 'tensor')
- grad_up: float32 [2048, 6144], P('fsdp', 'tensor')
- grad_down: float32 [2048, 6144], P('fsdp', 'tensor')
The draws below stay inside these ranges and needn't reach their ends.
Inputs may be any that keep to these rules, and one draw needn't show every extreme that they name: Each row gives the lengths of the 3 documents packed in order into one group's 2048 places; a row sums to 2048 and its largest length is 1024.
All inputs are finite; a program needn't handle non-finite values.
Results may differ from the reference program's by a relative error of at most 0.02.
Values may be sent and summed in bfloat16 or wider, within the bound.
No kernel may reach another device: no remote copies, remote signals or barrier semaphores. Data moves between devices by JAX's collectives and lax.ppermute only.
A program may use at most 320 MiB of HBM per device.

```python
import math
import jax
import jax.numpy as jnp
import numpy as np
from jax import lax

D = 2048
H = 16
KV = 8
HD = 128
FF = 6144
MAXLEN = 1024
DOCS = 3
GROUP_TOK = 2048
TOKENS = 8192
N_FSDP = 4


def level_of(own_key, extent, pieces, low, high):
    factor_of, own = 1.0, jax.random.fold_in(own_key, 6)
    for dim, parts in pieces:
        steps = jnp.exp(jax.random.uniform(jax.random.fold_in(own, dim), (parts,), jnp.float32, low / len(pieces), high / len(pieces)))
        factor_of = factor_of * jnp.repeat(steps, extent[dim] // parts).reshape([-1 if axis == dim else 1 for axis in range(len(extent))])
    return factor_of


def split_up(amount, total, reach, lean):
    weights = [(1 << 20) // math.isqrt(rank ** lean) + 1 for rank in range(2, amount + 1)]
    spare, counts = total - reach - (amount - 1), [1] * (amount - 1)
    while spare > 0:
        movable = [i for i in range(amount - 1) if counts[i] < reach]
        pool, left = sum([weights[i] for i in movable]), spare
        for i in movable:
            more = min(reach - counts[i], max(1, left * weights[i] // pool), spare)
            counts[i] = counts[i] + more
            spare = spare - more
    return np.array([reach] + counts)


def uneven(key, count, total, bound, skew):
    if count == 2:
        one = jax.random.randint(key, (), max(1, total - bound), min(bound, total - 1) + 1)
        return jnp.stack([one, total - one])
    tallies = jnp.asarray(split_up(count, total, bound, skew), jnp.int32)
    couples = (count - 1) // 2
    giver, receiver = tallies[1:1 + 2 * couples:2], tallies[2:2 + 2 * couples:2]
    room = jnp.minimum(giver - 1, bound - receiver)
    passed = jax.random.randint(jax.random.fold_in(key, 1), (couples,), 0, 1 << 20) % (room + 1)
    tallies = tallies.at[1:1 + 2 * couples:2].set(giver - passed).at[2:2 + 2 * couples:2].set(receiver + passed)
    return tallies[jax.random.permutation(jax.random.fold_in(key, 2), count)]


def noise(own_key, extent, width, limit, cuts=(), kind=jnp.bfloat16):
    values = jax.random.normal(own_key, extent, jnp.float32) * width
    if len(cuts) > 0:
        values = level_of(own_key, extent, cuts, -0.22, 0.18) * values
    return jnp.clip(values, min=-limit, max=limit).astype(kind)


def setup_inputs(seed: int = 0) -> dict:
    splits = jax.random.split(jax.random.key(seed), 15)
    return {
        "tokens": noise(splits[0], (TOKENS, D), 1.0, 6.0, ((0, 16),)),
        "lengths": jax.vmap(lambda own: uneven(own, DOCS, GROUP_TOK, MAXLEN, 2))(jax.random.split(splits[1], N_FSDP)).reshape((N_FSDP, DOCS)).astype(jnp.int32),
        "attn_gain": jnp.clip(1.0 + 0.1 * jax.random.normal(splits[2], (D,), jnp.float32), 0.5, 1.5).astype(jnp.bfloat16),
        "w_query": noise(splits[3], (D, H * HD), D ** -0.5, 0.125, ((0, 4), (1, 2))),
        "w_key": noise(splits[4], (D, KV * HD), D ** -0.5, 0.125, ((0, 4), (1, 2))),
        "w_value": noise(splits[5], (D, KV * HD), D ** -0.5, 0.125, ((0, 4), (1, 2))),
        "w_out": noise(splits[6], (D, H * HD), (H * HD // 16) ** -0.5, 0.5, ((0, 4), (1, 2))),
        "query_gain": jnp.clip(1.0 + 0.1 * jax.random.normal(splits[7], (HD,), jnp.float32), 0.5, 1.5).astype(jnp.bfloat16),
        "key_gain": jnp.clip(1.0 + 0.1 * jax.random.normal(splits[8], (HD,), jnp.float32), 0.5, 1.5).astype(jnp.bfloat16),
        "mlp_gain": jnp.clip(1.0 + 0.1 * jax.random.normal(splits[9], (D,), jnp.float32), 0.5, 1.5).astype(jnp.bfloat16),
        "w_gate": noise(splits[10], (D, FF), D ** -0.5, 0.125, ((0, 4), (1, 2))),
        "w_up": noise(splits[11], (D, FF), D ** -0.5, 0.125, ((0, 4), (1, 2))),
        "w_down": noise(splits[12], (D, FF), FF ** -0.5, 0.078125, ((0, 4), (1, 2))),
        "cotangent": noise(splits[13], (TOKENS, D), 1.0, 6.0, ((0, 16),)),
    }


EPS = 1e-06
THETA = 1000000.0
NEG = -1e+30

@jax.custom_vjp
def low(v):
    return lax.optimization_barrier(v.astype(jnp.bfloat16)).astype(jnp.float32)

@jax.custom_vjp
def low_back(v):
    return v

def low_keep(v):
    return (low(v), None)

def low_pass(kept, grad):
    return (grad,)

def back_keep(v):
    return (v, None)

def back_low(kept, grad):
    return (low(grad),)
low.defvjp(low_keep, low_pass)
low_back.defvjp(back_keep, back_low)

def rms_norm(values, gain):
    return values * lax.rsqrt(lax.optimization_barrier(jnp.mean(values * values, axis=-1, keepdims=True)) + EPS) * gain

def rotate(values, cosine, sine):
    half = values.shape[-1] // 2
    turned = jnp.concatenate([-values[..., half:], values[..., :half]], axis=-1)
    return values * cosine + turned * sine

def layout(lengths_row):
    starts = (jnp.cumsum(lengths_row) - lengths_row).astype(jnp.int32)
    places = jnp.arange(GROUP_TOK, dtype=jnp.int32)
    inside = starts[None, :] <= places[:, None]
    segment = (lax.optimization_barrier(jnp.sum(inside.astype(jnp.int32), axis=1)) - 1).astype(jnp.int32)
    first = lax.optimization_barrier(jnp.max(jnp.where(inside, starts[None, :], 0), axis=1)).astype(jnp.int32)
    return (segment, (places - first).astype(jnp.int32))

def rotary_tables(position, head_dim):
    exponent = jnp.arange(head_dim // 2, dtype=jnp.float32) * (2.0 / head_dim)
    inverse = THETA ** (-exponent)
    angle = position.astype(jnp.float32)[:, None] * inverse[None, :]
    angle = jnp.concatenate([angle, angle], axis=-1)
    return (jnp.cos(angle)[:, None, :], jnp.sin(angle)[:, None, :])

def attend_group(queries, keys, values, segment):
    group_rows = queries.shape[0]
    places = jnp.arange(group_rows, dtype=jnp.int32)
    allowed = (segment[:, None] == segment[None, :]) & (places[None, :] <= places[:, None])
    grouped = queries.reshape(group_rows, KV, H // KV, HD)
    raw_scores = low_back(jnp.einsum('qhgd,shd->hgqs', grouped, keys, precision=lax.Precision.HIGHEST))
    scores = jnp.where(allowed, raw_scores * HD ** (-0.5), NEG)
    row_top = lax.optimization_barrier(jnp.max(scores, axis=-1, keepdims=True))
    weights = jnp.exp(scores - row_top)
    probs = low(weights / lax.optimization_barrier(jnp.sum(weights, axis=-1, keepdims=True)))
    result = jnp.einsum('hgqs,shd->qhgd', probs, values, precision=lax.Precision.HIGHEST)
    return result.reshape(group_rows, H * HD)

def layer(inputs, attn_gain, w_query, w_key, w_value, w_out, query_gain, key_gain, mlp_gain, w_gate, w_up, w_down, segment, cosine, sine):
    rows = inputs.shape[0]
    highest = lax.Precision.HIGHEST
    normed = low(rms_norm(inputs, attn_gain))
    query_raw = low_back(jnp.dot(normed, w_query, precision=highest)).reshape(rows, H, HD)
    key_raw = low_back(jnp.dot(normed, w_key, precision=highest)).reshape(rows, KV, HD)
    values = low_back(low(jnp.dot(normed, w_value, precision=highest))).reshape(rows, KV, HD)
    queries = low_back(low(rotate(rms_norm(query_raw, query_gain), cosine, sine)))
    keys = low_back(low(rotate(rms_norm(key_raw, key_gain), cosine, sine)))
    groups = rows // GROUP_TOK
    checked = jax.checkpoint(attend_group)

    def one_group(packed):
        return checked(packed[0], packed[1], packed[2], packed[3])
    mixed = lax.map(one_group, (queries.reshape(groups, GROUP_TOK, H, HD), keys.reshape(groups, GROUP_TOK, KV, HD), values.reshape(groups, GROUP_TOK, KV, HD), segment.reshape(groups, GROUP_TOK)))
    context = low_back(low(mixed.reshape(rows, H * HD)))
    attended = inputs + low_back(jnp.dot(context, w_out.T, precision=highest))
    normed_two = low(rms_norm(attended, mlp_gain))
    gate = low_back(jnp.dot(normed_two, w_gate, precision=highest))
    up_proj = low_back(jnp.dot(normed_two, w_up, precision=highest))
    hidden = low(jax.nn.silu(gate) * up_proj)
    return attended + low_back(jnp.dot(hidden, w_down.T, precision=highest))

def reference(tokens, lengths, attn_gain, w_query, w_key, w_value, w_out, query_gain, key_gain, mlp_gain, w_gate, w_up, w_down, cotangent):
    segment, position = jax.vmap(layout)(lengths)
    segment = segment.reshape(-1)
    position = position.reshape(-1)
    cosine, sine = rotary_tables(position, HD)
    params = [array.astype(jnp.float32) for array in (tokens, attn_gain, w_query, w_key, w_value, w_out, query_gain, key_gain, mlp_gain, w_gate, w_up, w_down)]

    def forward(*params_in):
        return layer(*params_in, segment, cosine, sine)
    result, pullback = jax.vjp(forward, *params)
    grads = pullback(cotangent.astype(jnp.float32))
    return (result.astype(jnp.bfloat16), grads[0], grads[1], grads[2], grads[3], grads[4], grads[5], grads[6], grads[7], grads[8], grads[9], grads[10], grads[11])
```

```python
import functools

import jax
import jax.numpy as jnp
from jax import lax
from jax.experimental import pallas as pl
from jax.experimental.pallas import tpu as pltpu
from jax.sharding import PartitionSpec as P

EPS = 1e-06
THETA = 1000000.0
LOG2E = 1.4426950408889634
BF = jnp.bfloat16
F32 = jnp.float32


def dot_nn(left, right):
    return jnp.dot(left, right, preferred_element_type=F32)


def dot_nt(left, right):
    return lax.dot_general(left, right, (((1,), (1,)), ((), ())), preferred_element_type=F32)


def dot_tn(left, right):
    return lax.dot_general(left, right, (((0,), (0,)), ((), ())), preferred_element_type=F32)


def swap(value, axis, bits):
    size = lax.axis_size(axis)
    return lax.ppermute(value, axis, [(i, i ^ bits) for i in range(size)])


def ctx_gather(value):
    return [value] + [swap(value, "ctx", r) for r in range(1, lax.axis_size("ctx"))]


def ctx_scatter(parts):
    total = parts[0].astype(F32)
    for r in range(1, len(parts)):
        total = total + swap(parts[r].astype(BF), "ctx", r).astype(F32)
    return total


def sum_all(value, axis):
    size = lax.axis_size(axis)
    if size & (size - 1):
        return lax.psum(value, axis)
    step = 1
    while step < size:
        value = value + swap(value, axis, step)
        step *= 2
    return value


def pair_sum(own, other):
    arrived = swap(other().astype(BF), "tensor", 1)
    return (own() + arrived.astype(F32)).astype(BF)


def start_of(starts, places):
    first = jnp.zeros_like(places)
    for begin in starts:
        first = jnp.where(places >= begin, begin, first)
    return first


def head_norm(raw):
    factor = lax.rsqrt(jnp.mean(raw * raw, axis=-1, keepdims=True) + EPS)
    return raw * factor, factor


def turn(values, cosine, sine):
    return values * cosine + pltpu.roll(values, values.shape[-1] // 2, 1) * sine


def turn_back(values, cosine, sine):
    return values * cosine - pltpu.roll(values, values.shape[-1] // 2, 1) * sine


def rel_index(block, me, blocks):
    rel = block ^ me
    return (rel & 1) * (blocks // 2) + (rel >> 1)


def load_heads(meta, raws, gain_q, gain_k, cos_ref, sin_ref, q_s, k_s, v_s, ratio, hd):
    half = raws[0].shape[0]
    me = meta[0]
    for t_rel in range(2):
        for c_rel in range(half):
            block = (c_rel * 2 + t_rel) ^ me
            cosine, sine = cos_ref[block], sin_ref[block]
            for head in range(ratio):
                raw = raws[t_rel][c_rel, :, head * hd : (head + 1) * hd].astype(F32)
                q_s[block, head] = turn(head_norm(raw)[0] * gain_q[...], cosine, sine).astype(BF)
            raw = raws[t_rel][c_rel, :, ratio * hd : (ratio + 1) * hd].astype(F32)
            k_s[block] = turn(head_norm(raw)[0] * gain_k[...], cosine, sine).astype(BF)
            v_s[block] = raws[t_rel][c_rel, :, (ratio + 1) * hd : (ratio + 2) * hd]


def block_mask(i, j, starts, rows, blk):
    column = lax.broadcasted_iota(jnp.int32, (1, rows), 1)
    place = i * blk + lax.rem(column, blk)
    first = start_of(starts, place)
    key = j * blk + lax.broadcasted_iota(jnp.int32, (blk, rows), 0)
    return (key >= first) & (key <= place)


def first_block(i, starts, blk):
    place = i * blk
    first = jnp.int32(0)
    for begin in starts:
        first = jnp.where(place >= begin, begin, first)
    return first // blk


def attend_kernel(
    docs, meta, raw_a, raw_b, gain_q, gain_k, cos_ref, sin_ref, o_ref, lse_ref, q_s, k_s, v_s, vt_s
):
    blocks, ratio, blk, hd = q_s.shape
    rows = ratio * blk
    scale = hd ** (-0.5) * LOG2E
    me = meta[0]
    starts = [meta[1 + d] for d in range(1, docs)]
    load_heads(meta, (raw_a, raw_b), gain_q, gain_k, cos_ref, sin_ref, q_s, k_s, v_s, ratio, hd)
    for block in range(blocks):
        vt_s[block] = v_s[block].astype(F32).T.astype(BF)

    def per_query(i, carry):
        q = q_s[i].reshape(rows, hd)

        def per_key(j, state):
            total, acc = state
            scores = dot_nt(k_s[j], q) * scale
            weights = jnp.where(block_mask(i, j, starts, rows, blk), jnp.exp2(scores), 0.0)
            total = total + jnp.sum(weights, axis=0, keepdims=True)
            return total, acc + dot_nn(vt_s[j], weights.astype(BF))

        total, acc = lax.fori_loop(
            first_block(i, starts, blk),
            i + 1,
            per_key,
            (jnp.zeros((1, rows), F32), jnp.zeros((hd, rows), F32)),
        )
        out = (acc / total).T.astype(BF)
        where = rel_index(i, me, blocks)
        for head in range(ratio):
            o_ref[where, :, head * hd : (head + 1) * hd] = out[head * blk : (head + 1) * blk]
        lse_ref[i] = jnp.log2(total)
        return carry

    lax.fori_loop(0, blocks, per_query, 0)


def attend_back_kernel(
    docs,
    meta,
    raw_a,
    raw_b,
    do_a,
    do_b,
    o_ref,
    lse_ref,
    gain_q,
    gain_k,
    cos_ref,
    sin_ref,
    d_ref,
    gq_ref,
    gk_ref,
    q_s,
    k_s,
    v_s,
    kt_s,
    do_s,
    dq_s,
    dk_s,
    dv_s,
    delta_s,
):
    blocks, ratio, blk, hd = q_s.shape
    rows = ratio * blk
    scale = hd ** (-0.5)
    me = meta[0]
    half = blocks // 2
    starts = [meta[1 + d] for d in range(1, docs)]
    load_heads(meta, (raw_a, raw_b), gain_q, gain_k, cos_ref, sin_ref, q_s, k_s, v_s, ratio, hd)
    for block in range(blocks):
        kt_s[block] = k_s[block].astype(F32).T.astype(BF)
        dk_s[block] = jnp.zeros((blk, hd), F32)
        dv_s[block] = jnp.zeros((blk, hd), F32)
    for t_rel in range(2):
        source = (do_a, do_b)[t_rel]
        for c_rel in range(half):
            block = (c_rel * 2 + t_rel) ^ me
            for head in range(ratio):
                span = slice(head * hd, (head + 1) * hd)
                grad = source[c_rel, :, span]
                out = o_ref[t_rel * half + c_rel, :, span].astype(F32)
                do_s[block, head] = grad
                product = (grad.astype(F32) * out).T
                delta_s[block, :, head * blk : (head + 1) * blk] = jnp.sum(
                    product, axis=0, keepdims=True
                )

    def per_query(i, carry):
        q = q_s[i].reshape(rows, hd)
        grad = do_s[i].reshape(rows, hd)
        lse = lse_ref[i]
        delta = delta_s[i]

        def per_key(j, acc):
            scores = dot_nt(k_s[j], q) * (scale * LOG2E) - lse
            probs = jnp.where(block_mask(i, j, starts, rows, blk), jnp.exp2(scores), 0.0)
            grad_probs = dot_nt(v_s[j], grad)
            grad_scores = (probs * (grad_probs - delta) * scale).astype(BF)
            dv_s[j] += dot_nn(probs.astype(BF), grad)
            dk_s[j] += dot_nn(grad_scores, q)
            return acc + dot_nn(kt_s[j], grad_scores)

        acc = lax.fori_loop(
            first_block(i, starts, blk), i + 1, per_key, jnp.zeros((hd, rows), F32)
        )
        dq_s[i] = acc.T.reshape(ratio, blk, hd)
        return carry

    lax.fori_loop(0, blocks, per_query, 0)

    sum_q = jnp.zeros((1, hd), F32)
    sum_k = jnp.zeros((1, hd), F32)
    for t_rel in range(2):
        for c_rel in range(half):
            block = (c_rel * 2 + t_rel) ^ me
            cosine, sine = cos_ref[block], sin_ref[block]
            source = (raw_a, raw_b)[t_rel]
            for head in range(ratio + 1):
                span = slice(head * hd, (head + 1) * hd)
                unit, factor = head_norm(source[c_rel, :, span].astype(F32))
                grad = dq_s[block, head] if head < ratio else dk_s[block]
                grad = turn_back(grad, cosine, sine)
                total = jnp.sum(grad * unit, axis=0, keepdims=True)
                if head < ratio:
                    sum_q = sum_q + total
                    grad = grad * gain_q[...]
                else:
                    sum_k = sum_k + total
                    grad = grad * gain_k[...]
                mean = jnp.mean(grad * unit, axis=-1, keepdims=True)
                d_ref[t_rel * half + c_rel, :, span] = ((grad - unit * mean) * factor).astype(BF)
            span = slice((ratio + 1) * hd, (ratio + 2) * hd)
            d_ref[t_rel * half + c_rel, :, span] = dv_s[block].astype(BF)
    gq_ref[...] = sum_q
    gk_ref[...] = sum_k


def vmem_call(kernel, meta, arrays, outs, scratch, name):
    whole = pl.BlockSpec(memory_space=pltpu.VMEM)
    return pl.pallas_call(
        kernel,
        out_shape=outs,
        in_specs=[pl.BlockSpec(memory_space=pltpu.SMEM)] + [whole] * len(arrays),
        out_specs=jax.tree.map(lambda _: whole, outs),
        scratch_shapes=scratch,
        name=name,
    )(meta, *arrays)


def attend(docs, meta, raws, gains, tables, ratio, hd):
    half, blk, _ = raws[0].shape
    blocks = 2 * half
    rows = ratio * blk
    outs = (
        jax.ShapeDtypeStruct((blocks, blk, ratio * hd), BF),
        jax.ShapeDtypeStruct((blocks, 1, rows), F32),
    )
    scratch = [
        pltpu.VMEM((blocks, ratio, blk, hd), BF),
        pltpu.VMEM((blocks, blk, hd), BF),
        pltpu.VMEM((blocks, blk, hd), BF),
        pltpu.VMEM((blocks, hd, blk), BF),
    ]
    kernel = functools.partial(attend_kernel, docs)
    return vmem_call(kernel, meta, (*raws, *gains, *tables), outs, scratch, "attend")


def attend_back(docs, meta, raws, grads, out, lse, gains, tables, ratio, hd):
    half, blk, width = raws[0].shape
    blocks = 2 * half
    rows = ratio * blk
    outs = (
        jax.ShapeDtypeStruct((blocks, blk, width), BF),
        jax.ShapeDtypeStruct((1, hd), F32),
        jax.ShapeDtypeStruct((1, hd), F32),
    )
    scratch = [
        pltpu.VMEM((blocks, ratio, blk, hd), BF),
        pltpu.VMEM((blocks, blk, hd), BF),
        pltpu.VMEM((blocks, blk, hd), BF),
        pltpu.VMEM((blocks, hd, blk), BF),
        pltpu.VMEM((blocks, ratio, blk, hd), BF),
        pltpu.VMEM((blocks, ratio, blk, hd), F32),
        pltpu.VMEM((blocks, blk, hd), F32),
        pltpu.VMEM((blocks, blk, hd), F32),
        pltpu.VMEM((blocks, 1, rows), F32),
    ]
    kernel = functools.partial(attend_back_kernel, docs)
    return vmem_call(
        kernel, meta, (*raws, *grads, out, lse, *gains, *tables), outs, scratch, "attend_back"
    )


def spread_kernel(meta, *refs):
    pieces, factor, out = refs[:-2], refs[-2], refs[-1]
    step = pl.program_id(0)
    for r, piece in enumerate(pieces):

        @pl.when(step == r)
        def _():
            out[...] = piece[...].astype(F32) * factor[...]


def spread(me_ctx, pieces, factor, width, column):
    rows = pieces[0].shape[0]
    count = len(pieces)
    return pl.pallas_call(
        spread_kernel,
        out_shape=jax.ShapeDtypeStruct((rows, count * width), F32),
        grid_spec=pltpu.PrefetchScalarGridSpec(
            num_scalar_prefetch=1,
            grid=(count,),
            in_specs=[pl.BlockSpec((rows, width), lambda i, m: (0, column))] * count
            + [pl.BlockSpec((rows, 1), lambda i, m: (0, 0))],
            out_specs=pl.BlockSpec((rows, width), lambda i, m: (0, i ^ m[0])),
        ),
        name="spread",
    )(me_ctx, *pieces, factor)


def ctx_columns(weight, me_ctx, n_ctx):
    width = weight.shape[1] // n_ctx
    return lax.dynamic_slice_in_dim(weight, me_ctx * width, width, axis=1)


def join_halves(value, me_tensor):
    other = swap(value, "tensor", 1)
    first = jnp.where(me_tensor == 0, value, other)
    second = jnp.where(me_tensor == 0, other, value)
    return jnp.concatenate([first, second], axis=0)


def unit_rows(values):
    factor = lax.rsqrt(jnp.mean(values * values, axis=-1, keepdims=True) + EPS)
    return values * factor, factor


def unit_rows_back(grad, unit, factor):
    return factor * (grad - unit * jnp.mean(grad * unit, axis=-1, keepdims=True))


def on_device(
    tokens,
    lengths,
    attn_gain,
    w_query,
    w_key,
    w_value,
    w_out,
    query_gain,
    key_gain,
    mlp_gain,
    w_gate,
    w_up,
    w_down,
    cotangent,
):
    n_ctx = lax.axis_size("ctx")
    me_ctx = lax.axis_index("ctx")
    me_tensor = lax.axis_index("tensor")
    rows, width = tokens.shape
    blk = rows // lax.axis_size("tensor")
    blocks = 2 * n_ctx
    group_rows = rows * n_ctx
    hd = query_gain.shape[0]
    ratio = w_query.shape[1] // w_key.shape[1]
    docs = lengths.shape[1]
    half = n_ctx

    starts = jnp.cumsum(lengths[0]) - lengths[0]
    me = me_ctx * 2 + me_tensor
    meta = jnp.concatenate([me[None], starts]).astype(jnp.int32)
    ctx_meta = me_ctx[None].astype(jnp.int32)

    places = jnp.arange(group_rows, dtype=jnp.int32)
    inside = starts[None, :] <= places[:, None]
    position = places - jnp.max(jnp.where(inside, starts[None, :], 0), axis=1)
    exponent = jnp.arange(hd // 2, dtype=F32) * (2.0 / hd)
    angle = position.astype(F32)[:, None] * (THETA ** (-exponent))[None, :]
    cos_half, sin_half = jnp.cos(angle), jnp.sin(angle)
    tables = (
        jnp.concatenate([cos_half, cos_half], axis=-1).reshape(blocks, blk, hd),
        jnp.concatenate([-sin_half, sin_half], axis=-1).reshape(blocks, blk, hd),
    )
    gains = (query_gain.astype(F32).reshape(1, hd), key_gain.astype(F32).reshape(1, hd))
    attn_factor = attn_gain.astype(F32)[:, None]
    mlp_factor = mlp_gain.astype(F32)[:, None]

    def quarter(weight):
        return ctx_columns(weight, me_ctx, n_ctx)

    def fold(pieces, factor):
        return (jnp.concatenate(pieces, axis=1).astype(F32) * factor).astype(BF)

    def gathered(weight):
        own = lax.all_gather(weight, "fsdp", axis=0, tiled=True)
        return own, swap(own, "tensor", 1)

    qkv_own, qkv_other = gathered(
        fold([quarter(w_query), quarter(w_key), quarter(w_value)], attn_factor)
    )
    out_own, out_other = gathered(quarter(w_out))
    gu_own, gu_other = gathered(fold([quarter(w_gate), quarter(w_up)], mlp_factor))
    down_own, down_other = gathered(quarter(w_down))
    ff = down_own.shape[1]

    inputs = lax.dynamic_slice_in_dim(tokens, me_tensor * blk, blk).astype(F32)
    cot = lax.dynamic_slice_in_dim(cotangent, me_tensor * blk, blk)
    unit_one, factor_one = unit_rows(inputs)
    normed = jnp.concatenate(ctx_gather(unit_one.astype(BF)), axis=0)
    raw_other = dot_nn(normed, qkv_other).astype(BF)
    raw_own = dot_nn(normed, qkv_own).astype(BF)
    raws = (
        raw_own.reshape(half, blk, -1),
        swap(raw_other, "tensor", 1).reshape(half, blk, -1),
    )
    context, lse = attend(docs, meta, raws, gains, tables, ratio, hd)
    ctx_own = context[:half]
    ctx_other = swap(context[half:], "tensor", 1)
    attended = inputs + ctx_scatter(
        [dot_nt(ctx_own[r], out_own) + dot_nt(ctx_other[r], out_other) for r in range(n_ctx)]
    )

    cots = jnp.concatenate(ctx_gather(cot), axis=0)
    unit_two, factor_two = unit_rows(attended)
    normed_two = jnp.concatenate(ctx_gather(unit_two.astype(BF)), axis=0)

    def feed(weight):
        both = dot_nn(normed_two, weight)
        gate, up = both[:, :ff], both[:, ff:]
        sigma = jax.nn.sigmoid(gate)
        act = gate * sigma
        slope = up * sigma * (1.0 + gate * (1.0 - sigma))
        return (act * up).astype(BF), act.astype(BF), slope.astype(BF)

    hidden_own, act_own, slope_own = feed(gu_own)
    hidden_other, act_other, slope_other = feed(gu_other)
    block_rows = [slice(r * blk, (r + 1) * blk) for r in range(n_ctx)]
    mlp_out = ctx_scatter(
        [
            dot_nt(hidden_own[span], down_own) + dot_nt(hidden_other[span], down_other)
            for span in block_rows
        ]
    )
    layer_out = join_halves((attended + mlp_out).astype(BF), me_tensor)

    grad_down = pair_sum(lambda: dot_tn(cots, hidden_own), lambda: dot_tn(cots, hidden_other))

    def feed_back(weight, act, slope):
        grad = dot_nn(cots, weight)
        return jnp.concatenate(
            [(grad * slope.astype(F32)).astype(BF), (grad * act.astype(F32)).astype(BF)], axis=1
        )

    pre_own = feed_back(down_own, act_own, slope_own)
    pre_other = feed_back(down_other, act_other, slope_other)
    grad_unit_two = ctx_scatter(
        [
            dot_nt(pre_own[span], gu_own) + dot_nt(pre_other[span], gu_other)
            for span in block_rows
        ]
    )
    grad_gu = pair_sum(
        lambda: dot_tn(normed_two, pre_own), lambda: dot_tn(normed_two, pre_other)
    )
    sum_mlp = jnp.sum(grad_unit_two * unit_two, axis=0)
    grad_attended = cot.astype(F32) + unit_rows_back(grad_unit_two, unit_two, factor_two)
    branch = jnp.concatenate(ctx_gather(grad_attended.astype(BF)), axis=0)

    def scattered(grad):
        return lax.psum_scatter(grad, "fsdp", scatter_dimension=0, tiled=True)

    down_pieces = ctx_gather(scattered(grad_down))
    gu_pieces = ctx_gather(scattered(grad_gu))

    gctx_other = dot_nn(branch, out_other).astype(BF)
    gctx_own = dot_nn(branch, out_own).astype(BF)
    grads = (
        gctx_own.reshape(half, blk, -1),
        swap(gctx_other, "tensor", 1).reshape(half, blk, -1),
    )
    flat = (rows * n_ctx // 2, ratio * hd)
    grad_out = pair_sum(
        lambda: dot_tn(branch, ctx_own.reshape(flat)),
        lambda: dot_tn(branch, ctx_other.reshape(flat)),
    )
    out_pieces = ctx_gather(scattered(grad_out))
    d_raw, sum_q, sum_k = attend_back(
        docs, meta, raws, grads, context, lse, gains, tables, ratio, hd
    )
    d_own = d_raw[:half]
    d_other = swap(d_raw[half:], "tensor", 1)
    flat = (rows * n_ctx // 2, d_raw.shape[-1])
    grad_qkv = pair_sum(
        lambda: dot_tn(normed, d_own.reshape(flat)), lambda: dot_tn(normed, d_other.reshape(flat))
    )
    qkv_pieces = ctx_gather(scattered(grad_qkv))
    grad_unit_one = ctx_scatter(
        [dot_nt(d_own[r], qkv_own) + dot_nt(d_other[r], qkv_other) for r in range(n_ctx)]
    )
    sum_attn = jnp.sum(grad_unit_one * unit_one, axis=0)
    grad_tokens = join_halves(
        grad_attended + unit_rows_back(grad_unit_one, unit_one, factor_one), me_tensor
    )

    sums = jnp.concatenate([sum_attn, sum_mlp, sum_q[0], sum_k[0]]).reshape(-1, hd)
    for axis in ("tensor", "ctx", "fsdp"):
        sums = sum_all(sums, axis)
    sums = sums.reshape(-1)
    share = attn_gain.shape[0]
    offset = lax.axis_index("fsdp") * share
    grad_attn_gain = lax.dynamic_slice_in_dim(sums, offset, share) / attn_factor[:, 0]
    grad_mlp_gain = lax.dynamic_slice_in_dim(sums, width + offset, share) / mlp_factor[:, 0]
    grad_query_gain = sums[2 * width : 2 * width + hd]
    grad_key_gain = sums[2 * width + hd :]

    ones = jnp.ones_like(attn_factor)
    q_width = ratio * hd
    return (
        layer_out,
        grad_tokens,
        grad_attn_gain,
        spread(ctx_meta, qkv_pieces, attn_factor, q_width, 0),
        spread(ctx_meta, qkv_pieces, attn_factor, hd, ratio),
        spread(ctx_meta, qkv_pieces, attn_factor, hd, ratio + 1),
        spread(ctx_meta, out_pieces, ones, q_width, 0),
        grad_query_gain,
        grad_key_gain,
        grad_mlp_gain,
        spread(ctx_meta, gu_pieces, mlp_factor, ff, 0),
        spread(ctx_meta, gu_pieces, mlp_factor, ff, 1),
        spread(ctx_meta, down_pieces, ones, ff, 0),
    )


def solution(mesh):
    in_specs = (
        P(("fsdp", "ctx"), None),
        P("fsdp", None),
        P("fsdp"),
        P("fsdp", "tensor"),
        P("fsdp", "tensor"),
        P("fsdp", "tensor"),
        P("fsdp", "tensor"),
        P(),
        P(),
        P("fsdp"),
        P("fsdp", "tensor"),
        P("fsdp", "tensor"),
        P("fsdp", "tensor"),
        P(("fsdp", "ctx"), None),
    )
    out_specs = (
        P(("fsdp", "ctx"), None),
        P(("fsdp", "ctx"), None),
        P("fsdp"),
        P("fsdp", "tensor"),
        P("fsdp", "tensor"),
        P("fsdp", "tensor"),
        P("fsdp", "tensor"),
        P(),
        P(),
        P("fsdp"),
        P("fsdp", "tensor"),
        P("fsdp", "tensor"),
        P("fsdp", "tensor"),
    )
    return jax.shard_map(
        on_device, mesh=mesh, in_specs=in_specs, out_specs=out_specs, check_vma=False
    )
```
